32 devices in a mesh: fsdp: 16 (over z, y, x), tensor: 2 (over core).
Axes of the slice: x: 2, y: 2, z: 4, core: 2. Of those that a mesh axis runs over, the one named last changes fastest.
Arguments:
- tokens: bfloat16 [352, 8192], P('fsdp', 'tensor'), may hold values from -6 to 6
- gate_weight: bfloat16 [8192, 14336], P('tensor', 'fsdp'), may hold values from -0.0625 to 0.0625
- up_weight: bfloat16 [8192, 14336], P('tensor', 'fsdp'), may hold values from -0.0625 to 0.0625
- down_weight: bfloat16 [14336, 8192], P('fsdp', 'tensor'), may hold values from -0.375 to 0.375
Outputs:
- mixed: bfloat16 [352, 8192], P('fsdp', 'tensor')
- token_scale: float32 [352], P('tensor')
The draws below stay inside these ranges and needn't reach their ends.
All inputs are finite; a program needn't handle non-finite values. Where the reference program divides by a largest or mean magnitude, that divisor is 1e-20 or more.
Results may differ from the reference program's by a relative error of at most 0.0049.
Values may be sent and summed in bfloat16 or wider, within the bound.
No kernel may reach another device: no remote copies, remote signals or barrier semaphores. Data moves between devices by JAX's collectives and lax.ppermute only.
A program may use at most 64 MiB of HBM per device.

```python
import jax
import jax.numpy as jnp

D = 8192
FF_W = 14336
TOKENS = 352


def strengthened(result, rng, source, target, shards_of, factor):
    def block_of(position):
        return (jnp.arange(result.shape[position]) // (result.shape[position] // shards_of)).reshape((-1,) + (1,) * (result.ndim - 1 - position))

    near = jax.random.permutation(rng, shards_of)[block_of(target)]
    other_side = (block_of(target) + shards_of // 2) % shards_of
    return jnp.where((block_of(source) == near) | (block_of(source) == other_side), factor * result, result)


def level_of(rng, extent, shards, low, high):
    factor_of, own = 1.0, jax.random.fold_in(rng, 6)
    for dim, parts in shards:
        draws = jnp.exp(jax.random.uniform(jax.random.fold_in(own, dim), (parts,), jnp.float32, low / len(shards), high / len(shards)))
        factor_of = factor_of * jnp.repeat(draws, extent[dim] // parts).reshape([-1 if axis == dim else 1 for axis in range(len(extent))])
    return factor_of


def bell_draw(stream_key, shape, deviation, bound, shards=(), held_as=jnp.bfloat16):
    result = jax.random.normal(stream_key, shape, jnp.float32) * deviation
    if len(shards) > 0:
        result = level_of(stream_key, shape, shards, -0.22, 0.18) * result
    return jnp.clip(result, min=-bound, max=bound).astype(held_as)


def bell_draw_with(stream_key, dims, width, bound, pieces, heavy, held_as=jnp.bfloat16):
    array = width * jax.random.normal(stream_key, dims, jnp.float32)
    if pieces:
        array = array * level_of(stream_key, dims, pieces, -0.22, 0.18)
    return jnp.clip(strengthened(array, jax.random.fold_in(stream_key, 3), *heavy), -bound, bound).astype(held_as)


def setup_inputs(seed: int = 0) -> dict:
    seeds = jax.random.split(jax.random.key(seed), 5)
    return {
        "tokens": bell_draw_with(seeds[0], (TOKENS, D), 1.0, 6.0, ((0, 16), (1, 2)), (1, 0, 16, 2.0)),
        "gate_weight": bell_draw(seeds[1], (D, FF_W), D ** -0.5, 0.0625, ((0, 2), (1, 16))),
        "up_weight": bell_draw(seeds[2], (D, FF_W), D ** -0.5, 0.0625, ((0, 2), (1, 16))),
        "down_weight": bell_draw(seeds[3], (FF_W, D), (FF_W // 64) ** -0.5, 0.375, ((0, 16), (1, 2))),
    }


def reference(tokens, gate_weight, up_weight, down_weight):
    gate = jnp.dot(tokens, gate_weight, preferred_element_type=jnp.float32)
    up = jnp.dot(tokens, up_weight, preferred_element_type=jnp.float32)
    activation = jax.nn.silu(gate) * up
    token_scale = jnp.max(jnp.abs(activation), axis=1) + 1e-6
    quantized = (activation / token_scale[:, None]).astype(jnp.bfloat16)
    mixed = jnp.dot(quantized, down_weight, preferred_element_type=jnp.float32).astype(jnp.bfloat16)
    return mixed, token_scale
```

```python
import jax
import jax.numpy as jnp
from jax import lax
from jax.sharding import PartitionSpec as P

epsilon = 1e-06
both = ("fsdp", "tensor")


def build(devices, cores):
    planes = devices // 4

    def pairs(move):
        return [
            (f * cores + t, move(f, t % 2) * cores + t)
            for f in range(devices)
            for t in range(cores)
        ]

    ring = pairs(lambda f, c: (f + 4) % devices)
    inner = pairs(lambda f, c: f ^ (1 if c else 2))
    outer = pairs(lambda f, c: f ^ (2 if c else 1))

    def send(value, route):
        return lax.ppermute(value, both, route)

    def swap_middle(value, rows):
        return jnp.concatenate(
            [value[:rows], value[2 * rows : 3 * rows], value[rows : 2 * rows], value[3 * rows :]]
        )

    def over_cores(value, rows, color):
        if cores == 2:
            other = lax.ppermute(value, "tensor", [(0, 1), (1, 0)])
            return value + swap_middle(other, rows)
        same = jnp.where(color == 0, value, swap_middle(value, rows))
        total = lax.psum(same, "tensor")
        return jnp.where(color == 0, total, swap_middle(total, rows))

    def shards(tokens, gate_weight, up_weight, down_weight):
        own_rows, _ = tokens.shape
        rows = -(-own_rows // 8) * 8
        place = lax.axis_index("fsdp")
        part = lax.axis_index("tensor")
        color = part % 2
        ring_type = jnp.bfloat16 if planes <= 4 else jnp.float32

        held = jnp.pad(tokens, ((0, rows - own_rows), (0, 0)))
        gathered = []
        for plane in range(planes):
            if plane:
                held = send(held, ring)
            pair = jnp.concatenate([held, send(held, inner)])
            gathered.append(jnp.concatenate([pair, send(pair, outer)]))

        sums, peaks = [], []
        for plane in range(planes):
            gate = jnp.dot(gathered[plane], gate_weight, preferred_element_type=jnp.float32)
            up = jnp.dot(gathered[plane], up_weight, preferred_element_type=jnp.float32)
            gate = over_cores(gate, rows, color)
            up = over_cores(up, rows, color)
            activation = jax.nn.silu(gate) * up
            peaks.append(jnp.max(jnp.abs(activation), axis=1).reshape(4, rows))
            sums.append(
                jnp.dot(
                    activation.astype(jnp.bfloat16),
                    down_weight,
                    preferred_element_type=jnp.float32,
                )
            )

        total = None
        for step in range(planes):
            value = sums[(step + 1) % planes]
            far = send(value[2 * rows :].astype(jnp.bfloat16), outer)
            pair = value[: 2 * rows] + far.astype(jnp.float32)
            near = send(pair[rows:].astype(jnp.bfloat16), inner)
            one = pair[:rows] + near.astype(jnp.float32)
            total = one if total is None else one + total.astype(jnp.float32)
            if step < planes - 1:
                total = send(total.astype(ring_type), ring)

        k = jnp.arange(planes)[:, None, None]
        b = jnp.arange(2)[None, :, None]
        a = jnp.arange(2)[None, None, :]
        along_y = jnp.where(color == 0, a, b)
        along_x = jnp.where(color == 0, b, a)
        plane_of = (place // 4 + planes - k) % planes
        index = (plane_of * 4 + ((place % 4) ^ (along_y * 2 + along_x))).reshape(-1)
        peak = jnp.concatenate(peaks)
        hit = index[None, :, None] == jnp.arange(devices)[:, None, None]
        peak = jnp.max(jnp.where(hit, peak[None], 0.0), axis=1)
        if devices & (devices - 1) == 0:
            bit = 1
            while bit < devices:
                route = [(f, f ^ bit) for f in range(devices)]
                peak = jnp.maximum(peak, lax.ppermute(peak, "fsdp", route))
                bit *= 2
        else:
            peak = lax.pmax(peak, "fsdp")
        scale = peak[:, :own_rows] + epsilon
        own_scale = lax.dynamic_slice_in_dim(scale, place, 1, 0).reshape(own_rows, 1)
        mixed = (total[:own_rows] / own_scale).astype(jnp.bfloat16)
        share = devices * own_rows // cores
        token_scale = lax.dynamic_slice_in_dim(scale.reshape(-1), part * share, share, 0)
        return mixed, token_scale

    return shards


def solution(mesh):
    devices, cores = mesh.shape["fsdp"], mesh.shape["tensor"]
    return jax.shard_map(
        build(devices, cores),
        mesh=mesh,
        in_specs=(
            P("fsdp", "tensor"),
            P("tensor", "fsdp"),
            P("tensor", "fsdp"),
            P("fsdp", "tensor"),
        ),
        out_specs=(P("fsdp", "tensor"), P("tensor")),
        check_vma=False,
    )
```
